32 devices in a mesh: replica: 4 (over y, core), table: 8 (over z, x).
Axes of the slice: x: 2, y: 2, z: 4, core: 2. Of those that a mesh axis runs over, the one named last changes fastest.
Arguments:
- cache: float32 [768, 16384], P('table', 'replica'), may hold values from -6 to 6
- accum: float32 [768, 16384], P('table', 'replica'), may hold values from 0.5 to 8
- row_ids: int32 [4, 8, 128], P('replica'), may hold values from 0 to 4095
- lengths: int32 [4, 8], P('replica'), may hold values from 1 to 128, 614 in all within a row
- seq_slot: int32 [4, 8], P('replica'), may hold values from 0 to 7, each once within a row
- block_mask: int32 [4, 8, 2, 2], P('replica'), may hold values 0 or 1
- cotangent: bfloat16 [4, 1024, 768], P('replica', 'table'), may hold values from -6 to 6
- w_uqkv: bfloat16 [768, 3072], P('replica'), may hold values from -0.21875 to 0.21875
- w_out: bfloat16 [768, 768], P('replica'), may hold values from -0.21875 to 0.21875
- w2_accum: float32 [768, 768], P('replica', 'table'), may hold values from 81.92 to 8192
Outputs:
- cache_new: float32 [768, 16384], P('table', 'replica')
- accum_new: float32 [768, 16384], P('table', 'replica')
- w2_step: float32 [768, 768], P('replica', 'table')
The draws below stay inside these ranges and needn't reach their ends.
Inputs may be any that keep to these rules, and one draw needn't show every extreme that they name: `lengths`: in every replica group some sequence has length 128. `seq_slot`: each row names every slot once.
All inputs are finite; a program needn't handle non-finite values. No bound on the sum of `block_mask` on one device may be relied on, other than what follows from the above.
Results may differ from the reference program's by a relative error of at most 0.012.
Values may be sent and summed in bfloat16 or wider, within the bound.
A program may use at most 64 MiB of HBM per device.

```python
import math
from functools import partial
import jax
import jax.numpy as jnp
import numpy as np
from jax import lax

D = 768
HEADS = 12
HEAD_DIM = 64
BPS = 2
CACHE = 4096
SEQ_LEN = 128
SEQS = 8
N_REPLICA = 4


def touch_ends(drawn, own_key, low, high):
    place = [jax.random.randint(jax.random.fold_in(own_key, axis), (), 0, length) for axis, length in enumerate(drawn.shape)]
    main_axis = drawn.shape.index(max(drawn.shape))
    neighbour = place[:main_axis] + [(place[main_axis] + 1) % drawn.shape[main_axis]] + place[main_axis + 1:]
    return drawn.at[tuple(place)].set(low).at[tuple(neighbour)].set(high)


def block_scale(stream_key, shape, shards, least, high):
    factor_of, own = 1.0, jax.random.fold_in(stream_key, 6)
    for dim, shards_of in shards:
        steps = jnp.exp(jax.random.uniform(jax.random.fold_in(own, dim), (shards_of,), jnp.float32, least / len(shards), high / len(shards)))
        factor_of = factor_of * jnp.repeat(steps, shape[dim] // shards_of).reshape([-1 if axis == dim else 1 for axis in range(len(shape))])
    return factor_of


def cumulative_ranks(number_of, lean):
    weights = [(1 << 20) // math.isqrt(grade ** lean) + 1 for grade in range(1, number_of + 1)]
    deviation = 1 + sum(weights) // (1 << 30)
    return np.cumsum(np.array([max(1, weight // deviation) for weight in weights]))


def ranked_ids(rng, shape, count, lean):
    grid = cumulative_ranks(count, lean)
    ticket = jax.random.randint(jax.random.fold_in(rng, 1), shape, 0, int(grid[count - 1]))
    standing = jnp.searchsorted(jnp.asarray(grid, jnp.int32), ticket, side="right")
    return jax.random.permutation(jax.random.fold_in(rng, 2), count)[standing].astype(jnp.int32)


def split_up(count, total, bound, slope):
    weights = [(1 << 20) // math.isqrt(rank ** slope) + 1 for rank in range(2, count + 1)]
    spare, given = total - bound - (count - 1), [1] * (count - 1)
    while spare > 0:
        free = [i for i in range(count - 1) if given[i] < bound]
        pool, left = sum([weights[i] for i in free]), spare
        for i in free:
            addition = min(bound - given[i], max(1, left * weights[i] // pool), spare)
            given[i] = given[i] + addition
            spare = spare - addition
    return np.array([bound] + given)


def ragged(rng, number_of, total, reach, slope):
    if number_of == 2:
        one = jax.random.randint(rng, (), max(1, total - reach), min(reach, total - 1) + 1)
        return jnp.stack([one, total - one])
    tallies = jnp.asarray(split_up(number_of, total, reach, slope), jnp.int32)
    pairs = (number_of - 1) // 2
    donor, sink = tallies[1:1 + 2 * pairs:2], tallies[2:2 + 2 * pairs:2]
    room = jnp.minimum(donor - 1, reach - sink)
    passed = jax.random.randint(jax.random.fold_in(rng, 1), (pairs,), 0, 1 << 20) % (room + 1)
    tallies = tallies.at[1:1 + 2 * pairs:2].set(donor - passed).at[2:2 + 2 * pairs:2].set(sink + passed)
    return tallies[jax.random.permutation(jax.random.fold_in(rng, 2), number_of)]


def bell_draw(key, extent, width, limit, cuts=(), held_as=jnp.bfloat16):
    result = jax.random.normal(key, extent, jnp.float32) * width
    if len(cuts) > 0:
        result = block_scale(key, extent, cuts, -0.22, 0.18) * result
    return jnp.clip(result, min=-limit, max=limit).astype(held_as)


def setup_inputs(seed: int = 0) -> dict:
    key_of = jax.random.split(jax.random.key(seed), 11)
    cache = bell_draw(key_of[0], (D, CACHE * N_REPLICA), 1.0, 6.0, ((0, 8), (1, 4)), jnp.float32)
    accum = jnp.clip(jnp.exp(math.log(8.0) - 2.7725887 * jax.random.uniform(key_of[1], (D, CACHE * N_REPLICA), jnp.float32) ** block_scale(key_of[1], (D, CACHE * N_REPLICA), ((0, 8), (1, 4)), -0.2, 0.2)), 0.5, 8.0)
    row_ids = touch_ends(ranked_ids(key_of[2], (N_REPLICA, SEQS, SEQ_LEN), CACHE, 2), jax.random.fold_in(key_of[2], 3), 0, CACHE - 1).astype(jnp.int32)
    lengths = jax.vmap(lambda own: ragged(own, SEQS, SEQS * SEQ_LEN * 3 // 5, SEQ_LEN, 2))(jax.random.split(key_of[3], N_REPLICA)).reshape((N_REPLICA, SEQS)).astype(jnp.int32)
    seq_slot = jax.vmap(lambda own: jax.random.permutation(own, SEQS))(jax.random.split(key_of[4], N_REPLICA)).reshape((N_REPLICA, SEQS)).astype(jnp.int32)
    block_mask = touch_ends((jax.random.randint(key_of[5], (N_REPLICA, SEQS, BPS, BPS), 0, 4) < 3).astype(jnp.int32), jax.random.fold_in(key_of[5], 1), 0, 1)
    cotangent = bell_draw(key_of[6], (N_REPLICA, SEQS * SEQ_LEN, D), 1.0, 6.0, ((0, 4), (1, 8)))
    w_uqkv = bell_draw(key_of[7], (D, 4 * D), D ** -0.5, 0.21875, ((0, 4),))
    w_out = bell_draw(key_of[8], (D, D), D ** -0.5, 0.21875, ((0, 4),))
    w2_accum = jnp.clip(jnp.exp(math.log(8192.0) - 4.6051702 * jax.random.uniform(key_of[9], (D, D), jnp.float32) ** block_scale(key_of[9], (D, D), ((0, 4), (1, 8)), -0.2, 0.2)), 81.92, 8192.0)
    return dict(cache=cache, accum=accum, row_ids=row_ids, lengths=lengths, seq_slot=seq_slot, block_mask=block_mask, cotangent=cotangent, w_uqkv=w_uqkv, w_out=w_out, w2_accum=w2_accum)


EPS_NORM = 1e-05
EPS_ATTN = 1e-06
STEP_SIZE = 0.5

def normalize(row_data):
    centred = row_data - lax.optimization_barrier(jnp.mean(row_data, axis=-1, keepdims=True))
    variance = lax.optimization_barrier(jnp.mean(centred * centred, axis=-1, keepdims=True))
    return centred / jnp.sqrt(variance + EPS_NORM)

def pattern_mask(lengths_at, blocks_at, seq_len):
    block_count = blocks_at.shape[-1]
    block_width = seq_len // block_count
    places = jnp.arange(seq_len, dtype=jnp.int32)
    block_of = places // block_width
    same_block = block_of[:, None] == block_of[None, :]
    chosen = jnp.repeat(jnp.repeat(blocks_at, block_width, axis=1), block_width, axis=2) > 0
    chosen = chosen | same_block[None]
    causal = places[None, :] <= places[:, None]
    inside = places[None, :] < lengths_at[:, None]
    allowed = chosen & causal[None] & inside[:, :, None] & inside[:, None, :]
    return (allowed.astype(jnp.float32), inside)

def attention_branch(hidden_pre, allowed):
    slot_count = allowed.shape[0]
    seq_len = allowed.shape[1]
    projected = jax.nn.silu(hidden_pre).astype(jnp.bfloat16)
    gate_u = projected[:, :D]
    queries = projected[:, D:2 * D].reshape(slot_count, seq_len, HEADS, HEAD_DIM).astype(jnp.float32)
    key_rows = projected[:, 2 * D:3 * D].reshape(slot_count, seq_len, HEADS, HEAD_DIM).astype(jnp.float32)
    value_rows = projected[:, 3 * D:].reshape(slot_count, seq_len, HEADS, HEAD_DIM).astype(jnp.float32)
    scores = jnp.einsum('sihd,sjhd->shij', queries, key_rows) * HEAD_DIM ** (-0.5)
    weights = (jax.nn.silu(scores) * allowed[:, None]).astype(jnp.bfloat16)
    attended = jnp.einsum('shij,sjhd->sihd', weights.astype(jnp.float32), value_rows)
    attended = attended.reshape(slot_count * seq_len, D)
    centred_att = attended - lax.optimization_barrier(jnp.mean(attended, axis=-1, keepdims=True))
    inverse_dev = 1.0 / jnp.sqrt(lax.optimization_barrier(jnp.mean(centred_att * centred_att, axis=-1, keepdims=True)) + EPS_ATTN)
    return centred_att * inverse_dev * gate_u.astype(jnp.float32)

def group_step(summed, inputs):
    cache_part, accum_part, ids_part, lengths_part, slot_part, mask_part, cot_part, w_uqkv, w_out = inputs
    sequence_ids = jnp.arange(SEQS, dtype=jnp.int32)
    matches = (slot_part[:, None] == sequence_ids[None, :]).astype(jnp.int32)
    seq_at = lax.optimization_barrier(jnp.sum(sequence_ids[:, None] * matches, axis=0)).astype(jnp.int32)
    lengths_at = lax.optimization_barrier(jnp.sum(lengths_part[:, None] * matches, axis=0)).astype(jnp.int32)
    slot_ids = ids_part[seq_at].reshape(-1).astype(jnp.int32)
    blocks_at = mask_part[seq_at]
    allowed, inside = pattern_mask(lengths_at, blocks_at, SEQ_LEN)
    embedded = jnp.take(cache_part, slot_ids, axis=1).astype(jnp.bfloat16).T
    row_float = embedded.astype(jnp.float32)
    normed = normalize(row_float).astype(jnp.bfloat16)
    hidden_pre = jnp.dot(normed, w_uqkv, preferred_element_type=jnp.float32)
    live_cot = cot_part * inside.reshape(-1)[:, None].astype(jnp.bfloat16)
    d_gated = lax.dot_general(live_cot, w_out, (((1,), (1,)), ((), ())), preferred_element_type=jnp.float32)
    gated_raw, branch_vjp = jax.vjp(partial(attention_branch, allowed=allowed), hidden_pre)
    gated = gated_raw.astype(jnp.bfloat16)
    d_hidden = branch_vjp(d_gated)[0].astype(jnp.bfloat16)
    d_normed = lax.dot_general(d_hidden, w_uqkv, (((1,), (1,)), ((), ())), preferred_element_type=jnp.float32)
    _, norm_vjp = jax.vjp(normalize, row_float)
    row_grad = live_cot.astype(jnp.float32) + norm_vjp(d_normed)[0]
    grad_table = jnp.zeros((CACHE, D), jnp.float32).at[slot_ids].add(row_grad)
    grad_cols = grad_table.T
    accum_next = accum_part + grad_cols * grad_cols
    cache_next = cache_part - STEP_SIZE * grad_cols / jnp.sqrt(accum_next)
    weight_grad = lax.dot_general(gated, live_cot, (((0,), (0,)), ((), ())), preferred_element_type=jnp.float32)
    return (summed + weight_grad, (cache_next, accum_next))

def reference(cache, accum, row_ids, lengths, seq_slot, block_mask, cotangent, w_uqkv, w_out, w2_accum):
    cache_groups = cache.reshape(D, N_REPLICA, CACHE).transpose(1, 0, 2)
    accum_groups = accum.reshape(D, N_REPLICA, CACHE).transpose(1, 0, 2)
    count = N_REPLICA

    def step_one(summed, inputs):
        return group_step(summed, inputs + (w_uqkv, w_out))
    summed, stacked = lax.scan(step_one, jnp.zeros((D, D), jnp.float32), (cache_groups, accum_groups, row_ids, lengths, seq_slot, block_mask, cotangent))
    cache_new = stacked[0].transpose(1, 0, 2).reshape(D, count * CACHE)
    accum_new = stacked[1].transpose(1, 0, 2).reshape(D, count * CACHE)
    w2_step = summed / jnp.sqrt(w2_accum + summed * summed)
    return (cache_new, accum_new, w2_step)
```

```python
import functools

import jax
import jax.numpy as jnp
from jax import lax
from jax.experimental import pallas as pl
from jax.experimental.pallas import tpu as pltpu
from jax.sharding import PartitionSpec as P

D = 768
HEADS = 12
HEAD_DIM = 64
EPS_NORM = 1e-05
EPS_ATTN = 1e-06
STEP_SIZE = 0.5
PAIR = 2 * HEAD_DIM
CHUNK = 512

F32 = jnp.float32
BF16 = jnp.bfloat16

NN = (((1,), (0,)), ((), ()))
NT = (((1,), (1,)), ((), ()))
TN = (((0,), (0,)), ((), ()))


def mm(a, b, dims):
    return lax.dot_general(a, b, dims, preferred_element_type=F32)


def one_hot(ids, base, size):
    rows = lax.broadcasted_iota(jnp.int32, (size, ids.shape[1]), 0) + base
    return jnp.where(rows == ids, 1.0, 0.0).astype(BF16)


def layer_kernel(
    reps, tabs, blocks,
    meta, cache_hbm, ids_ref, cot_ref, w_hbm, wo_hbm,
    back_ref, grad_ref,
    cache_v, w_v, wo_v, picked, arrived, emb, normed, hid, proj, att, scores, wts,
    d_att, d_hid, live_cot, gsum, gsend, grecv, gt, tsend, trecv, rowg, rsend, rrecv,
    local_sem, w_s, w_r, wo_s, wo_r, e_s, e_r, g_s, g_r, t_s, t_r, b_s, b_r,
):
    rep = lax.axis_index("replica")
    tab = lax.axis_index("table")
    rows = w_hbm.shape[0]
    cols = cache_hbm.shape[0]
    seq = cot_ref.shape[0]

    def rep_at(i):
        return lax.rem(rep + i, reps)

    def tab_at(i):
        return lax.rem(tab + i, tabs)

    def row_block(r):
        return pl.ds(pl.multiple_of(r * rows, rows), rows)

    own_cache = pltpu.make_async_copy(cache_hbm, cache_v, local_sem.at[0])
    own_w = pltpu.make_async_copy(w_hbm, w_v.at[row_block(rep)], local_sem.at[1])
    own_wo = pltpu.make_async_copy(wo_hbm, wo_v.at[row_block(rep)], local_sem.at[2])
    own_cache.start()
    own_w.start()
    own_wo.start()

    barrier = pltpu.get_barrier_semaphore()

    @pl.loop(1, reps)
    def _(i):
        pl.semaphore_signal(barrier, inc=1, device_id={"replica": rep_at(i)})

    @pl.loop(1, tabs)
    def _(i):
        pl.semaphore_signal(barrier, inc=1, device_id={"table": tab_at(i)})

    pl.semaphore_wait(barrier, reps - 1 + tabs - 1)

    def w_copy(to, source):
        return pltpu.make_async_remote_copy(
            src_ref=w_hbm, dst_ref=w_v.at[row_block(source)],
            send_sem=w_s.at[to], recv_sem=w_r.at[source], device_id={"replica": to})

    def wo_copy(to, source):
        return pltpu.make_async_remote_copy(
            src_ref=wo_hbm, dst_ref=wo_v.at[row_block(source)],
            send_sem=wo_s.at[to], recv_sem=wo_r.at[source], device_id={"replica": to})

    def g_copy(to, source):
        return pltpu.make_async_remote_copy(
            src_ref=gsend.at[row_block(to)], dst_ref=grecv.at[source],
            send_sem=g_s.at[to], recv_sem=g_r.at[source], device_id={"replica": to})

    def e_copy(to, source):
        return pltpu.make_async_remote_copy(
            src_ref=picked.at[to], dst_ref=arrived.at[source],
            send_sem=e_s.at[to], recv_sem=e_r.at[source], device_id={"table": to})

    def t_copy(to, source):
        return pltpu.make_async_remote_copy(
            src_ref=tsend.at[to], dst_ref=trecv.at[source],
            send_sem=t_s.at[to], recv_sem=t_r.at[source], device_id={"table": to})

    def b_copy(to, source):
        return pltpu.make_async_remote_copy(
            src_ref=rsend.at[to], dst_ref=rrecv.at[source],
            send_sem=b_s.at[to], recv_sem=b_r.at[source], device_id={"table": to})

    def start_rep(copy):
        @pl.loop(1, reps)
        def _(i):
            copy(rep_at(i), rep).start()

    def start_tab(copy):
        @pl.loop(1, tabs)
        def _(i):
            copy(tab_at(i), tab).start()

    def recv_tab(copy):
        @pl.loop(1, tabs)
        def _(i):
            copy(tab, tab_at(i)).wait_recv()

    start_rep(w_copy)
    start_rep(wo_copy)

    length = meta[0]
    width = seq // blocks
    at_i = lax.broadcasted_iota(jnp.int32, (seq, seq), 0)
    at_j = lax.broadcasted_iota(jnp.int32, (seq, seq), 1)
    pattern = jnp.zeros((seq, seq), jnp.int32)
    for a in range(blocks):
        for b in range(blocks):
            here = ((at_i >= a * width) & (at_i < (a + 1) * width)
                    & (at_j >= b * width) & (at_j < (b + 1) * width))
            chosen = 1 if a == b else meta[1 + a * blocks + b]
            pattern = jnp.where(here, chosen, pattern)
    allowed = jnp.where((pattern > 0) & (at_j <= at_i) & (at_i < length), 1.0, 0.0)
    live = jnp.where(lax.broadcasted_iota(jnp.int32, (seq, D), 0) < length, 1.0, 0.0)
    cot = cot_ref[...].astype(F32) * live
    live_cot[...] = cot.astype(BF16)

    own_cache.wait()
    ids = ids_ref[...]
    size = min(CHUNK, cache_v.shape[1])
    found = jnp.zeros((cols, ids.shape[1]), F32)
    for m in range(0, cache_v.shape[1], size):
        found = found + mm(
            cache_v[:, m : m + size].astype(BF16), one_hot(ids, m, size), NN)
    for q in range(tabs):
        picked[q] = found[:, q * seq : (q + 1) * seq].astype(BF16)
    start_tab(e_copy)
    arrived[tab] = picked[tab]
    recv_tab(e_copy)
    for q in range(tabs):
        emb[q * cols : (q + 1) * cols, :] = arrived[q].astype(F32)

    e = emb[...]
    centred = e - jnp.mean(e, axis=0, keepdims=True)
    inverse = 1.0 / jnp.sqrt(jnp.mean(centred * centred, axis=0, keepdims=True) + EPS_NORM)
    norm = centred * inverse
    normed[...] = norm.astype(BF16)

    own_w.wait()
    hid[...] = mm(normed[row_block(rep), :], w_v[row_block(rep), :], TN)

    @pl.loop(1, reps)
    def _(i):
        source = rep_at(i)
        w_copy(rep, source).wait_recv()
        hid[...] += mm(normed[row_block(source), :], w_v[row_block(source), :], TN)

    for c in range(0, 4 * D, D):
        h = hid[:, c : c + D]
        proj[:, c : c + D] = (h / (1.0 + jnp.exp(-h))).astype(BF16)

    lane = lax.broadcasted_iota(jnp.int32, (seq, PAIR), 1)
    halves = [lane < HEAD_DIM, lane >= HEAD_DIM]

    def half(x, k):
        return jnp.where(halves[k], x, jnp.zeros_like(x))

    scale = HEAD_DIM ** (-0.5)
    for p in range(HEADS // 2):
        at = p * PAIR
        q2 = proj[:, D + at : D + at + PAIR]
        k2 = proj[:, 2 * D + at : 2 * D + at + PAIR]
        v2 = proj[:, 3 * D + at : 3 * D + at + PAIR]
        total = None
        for k in range(2):
            s = mm(q2, half(k2, k), NT) * scale
            scores[2 * p + k] = s
            w = (s / (1.0 + jnp.exp(-s)) * allowed).astype(BF16)
            wts[2 * p + k] = w
            part = mm(w, half(v2, k), NN)
            total = part if total is None else total + part
        att[:, at : at + PAIR] = total

    a = att[...]
    c_att = a - jnp.mean(a, axis=1, keepdims=True)
    inv_att = 1.0 / jnp.sqrt(jnp.mean(c_att * c_att, axis=1, keepdims=True) + EPS_ATTN)
    y = c_att * inv_att
    gate = proj[:, :D].astype(F32)
    gated = (y * gate).astype(BF16)

    gsum[...] = mm(gated, live_cot[...], TN)
    gsend[...] = gsum[...].astype(BF16)
    start_rep(g_copy)

    own_wo.wait()

    @pl.loop(1, reps)
    def _(i):
        wo_copy(rep, rep_at(i)).wait_recv()

    d_gated = mm(live_cot[...], wo_v[...], NT)

    def silu_grad(v):
        sig = 1.0 / (1.0 + jnp.exp(-v))
        return sig * (1.0 + v * (1.0 - sig))

    def put(at, width_of, value):
        h = hid[:, at : at + width_of]
        d_hid[:, at : at + width_of] = (
            value.astype(BF16).astype(F32) * silu_grad(h)).astype(BF16)

    put(0, D, d_gated * y)
    d_y = d_gated * gate
    d_att[...] = (inv_att * (
        d_y - jnp.mean(d_y, axis=1, keepdims=True)
        - y * jnp.mean(d_y * y, axis=1, keepdims=True))).astype(BF16)

    for p in range(HEADS // 2):
        at = p * PAIR
        q2 = proj[:, D + at : D + at + PAIR]
        k2 = proj[:, 2 * D + at : 2 * D + at + PAIR]
        v2 = proj[:, 3 * D + at : 3 * D + at + PAIR]
        da2 = d_att[:, at : at + PAIR]
        dq = dk = dv = None
        for k in range(2):
            s = scores[2 * p + k]
            dw = mm(da2, half(v2, k), NT).astype(BF16).astype(F32)
            ds = (dw * allowed * silu_grad(s) * scale).astype(BF16)
            dv_k = mm(wts[2 * p + k], half(da2, k), TN)
            dq_k = mm(ds, half(k2, k), NN)
            dk_k = mm(ds, half(q2, k), TN)
            dq = dq_k if dq is None else dq + dq_k
            dk = dk_k if dk is None else dk + dk_k
            dv = dv_k if dv is None else dv + dv_k
        put(D + at, PAIR, dq)
        put(2 * D + at, PAIR, dk)
        put(3 * D + at, PAIR, dv)

    d_norm = mm(w_v[...], d_hid[...], NT)
    e = emb[...]
    centred = e - jnp.mean(e, axis=0, keepdims=True)
    inverse = 1.0 / jnp.sqrt(jnp.mean(centred * centred, axis=0, keepdims=True) + EPS_NORM)
    norm = centred * inverse
    rowg[...] = live_cot[...].astype(F32).T + inverse * (
        d_norm - jnp.mean(d_norm, axis=0, keepdims=True)
        - norm * jnp.mean(d_norm * norm, axis=0, keepdims=True))
    for q in range(tabs):
        rsend[q] = rowg[q * cols : (q + 1) * cols, :].astype(BF16)
    start_tab(b_copy)
    rrecv[tab] = rsend[tab]

    summed = gsum[row_block(rep), :]
    for i in range(1, reps):
        source = rep_at(i)
        g_copy(rep, source).wait_recv()
        summed = summed + grecv[source].astype(F32)
    gt[...] = summed.T
    for q in range(tabs):
        tsend[q] = gt[q * cols : (q + 1) * cols, :].astype(BF16)
    start_tab(t_copy)
    trecv[tab] = tsend[tab]

    recv_tab(b_copy)
    back_ref[...] = rrecv[...]

    recv_tab(t_copy)
    out = trecv[0].astype(F32)
    for q in range(1, tabs):
        out = out + trecv[q].astype(F32)
    grad_ref[...] = out

    for copy in (w_copy, wo_copy, g_copy):
        @pl.loop(1, reps)
        def _(i):
            copy(rep_at(i), rep).wait_send()

    for copy in (e_copy, b_copy, t_copy):
        @pl.loop(1, tabs)
        def _(i):
            copy(tab_at(i), tab).wait_send()


def update_kernel(back_ref, ids_ref, cache_ref, accum_ref, cache_out, accum_out, grads):
    step = pl.program_id(0)
    tabs, _, seq = back_ref.shape
    size = cache_ref.shape[1]

    @pl.when(step == 0)
    def _():
        for q in range(tabs):
            grads[:, q * seq : (q + 1) * seq] = back_ref[q]

    grad = mm(grads[...], one_hot(ids_ref[...], step * size, size), NT)
    accum_next = accum_ref[...] + grad * grad
    accum_out[...] = accum_next
    cache_out[...] = cache_ref[...] - STEP_SIZE * grad / jnp.sqrt(accum_next)


def body(cache, accum, row_ids, lengths, seq_slot, block_mask, cotangent, w_uqkv, w_out, w2_accum):
    reps = lax.axis_size("replica")
    tabs = lax.axis_size("table")
    tab = lax.axis_index("table")
    cols, cached = cache.shape
    rows = w_uqkv.shape[0]
    seq = row_ids.shape[2]
    blocks = block_mask.shape[-1]
    slots = seq_slot.shape[1]

    slot = jnp.arange(slots, dtype=jnp.int32)
    match = seq_slot[0][None, :] == slot[:, None]
    ids = jnp.sum(jnp.where(match[:, :, None], row_ids[0][None], 0), axis=1)
    ids = ids.reshape(1, slots * seq)
    own = seq_slot[0] == tab
    facts = jnp.concatenate(
        [lengths[0][:, None], block_mask[0].reshape(slots, blocks * blocks)], axis=1)
    meta = jnp.sum(jnp.where(own[:, None], facts, 0), axis=0)

    vmem = pl.BlockSpec(memory_space=pltpu.VMEM)
    smem = pl.BlockSpec(memory_space=pltpu.SMEM)
    hbm = pl.BlockSpec(memory_space=pl.ANY)
    dma = pltpu.SemaphoreType.DMA
    V = pltpu.VMEM
    back, grad_t = pl.pallas_call(
        functools.partial(layer_kernel, reps, tabs, blocks),
        out_shape=(
            jax.ShapeDtypeStruct((tabs, cols, seq), BF16),
            jax.ShapeDtypeStruct((cols, rows), F32),
        ),
        in_specs=[smem, hbm, vmem, vmem, hbm, hbm],
        out_specs=(vmem, vmem),
        scratch_shapes=[
            V((cols, cached), F32), V((D, 4 * D), BF16), V((D, D), BF16),
            V((tabs, cols, seq), BF16), V((tabs, cols, seq), BF16), V((D, seq), F32),
            V((D, seq), BF16), V((seq, 4 * D), F32), V((seq, 4 * D), BF16),
            V((seq, D), F32), V((HEADS, seq, seq), F32), V((HEADS, seq, seq), BF16),
            V((seq, D), BF16), V((seq, 4 * D), BF16), V((seq, D), BF16),
            V((D, D), F32), V((D, D), BF16), V((reps, rows, D), BF16),
            V((D, rows), F32), V((tabs, cols, rows), BF16), V((tabs, cols, rows), BF16),
            V((D, seq), F32), V((tabs, cols, seq), BF16), V((tabs, cols, seq), BF16),
            dma((3,)), dma((reps,)), dma((reps,)), dma((reps,)), dma((reps,)),
            dma((tabs,)), dma((tabs,)), dma((reps,)), dma((reps,)),
            dma((tabs,)), dma((tabs,)), dma((tabs,)), dma((tabs,)),
        ],
        compiler_params=pltpu.CompilerParams(
            collective_id=0, has_side_effects=True, vmem_limit_bytes=56 * 1024 * 1024),
        name="layer",
    )(meta, cache, ids, cotangent[0], w_uqkv, w_out)

    size = min(CHUNK, cached)
    block = pl.BlockSpec((cols, size), lambda m: (0, m))
    cache_next, accum_next = pl.pallas_call(
        update_kernel,
        grid=(cached // size,),
        out_shape=(jax.ShapeDtypeStruct(cache.shape, F32),) * 2,
        in_specs=[
            pl.BlockSpec((tabs, cols, seq), lambda m: (0, 0, 0)),
            pl.BlockSpec((1, slots * seq), lambda m: (0, 0)),
            block, block,
        ],
        out_specs=(block, block),
        scratch_shapes=[V((cols, tabs * seq), BF16)],
        compiler_params=pltpu.CompilerParams(vmem_limit_bytes=40 * 1024 * 1024),
        name="update",
    )(back, ids, cache, accum)

    summed = grad_t.T
    w2_step = summed / jnp.sqrt(w2_accum + summed * summed)
    return (cache_next, accum_next, w2_step)


def solution(mesh):
    return jax.shard_map(
        body,
        mesh=mesh,
        in_specs=(
            P("table", "replica"),
            P("table", "replica"),
            P("replica", None, None),
            P("replica", None),
            P("replica", None),
            P("replica", None, None, None),
            P("replica", "table", None),
            P("replica", None),
            P("replica", None),
            P("replica", "table"),
        ),
        out_specs=(P("table", "replica"), P("table", "replica"), P("replica", "table")),
        check_vma=False,
    )
```

```python
import functools

import jax
import jax.numpy as jnp
from jax import lax
from jax.experimental import pallas as pl
from jax.experimental.pallas import tpu as pltpu
from jax.sharding import PartitionSpec as P

D = 768
HEADS = 12
HEAD_DIM = 64
EPS_NORM = 1e-05
EPS_ATTN = 1e-06
STEP_SIZE = 0.5
PAIR = 2 * HEAD_DIM
CHUNK = 512
PIECE = D // 2

F32 = jnp.float32
BF16 = jnp.bfloat16

NN = (((1,), (0,)), ((), ()))
NT = (((1,), (1,)), ((), ()))
TN = (((0,), (0,)), ((), ()))


def mm(a, b, dims):
    return lax.dot_general(a, b, dims, preferred_element_type=F32)


def one_hot(ids, base, size):
    rows = lax.broadcasted_iota(jnp.int32, (size, ids.shape[1]), 0) + base
    return jnp.where(rows == ids, 1.0, 0.0).astype(BF16)


def layer_kernel(
    reps, tabs, blocks,
    slots_ref, lengths_ref, mask_ref, cache_hbm, row_ids_ref, cot_ref, w_hbm, wo_hbm,
    back_ref, grad_ref, ids_ref,
    cache_v, w_v, picked, arrived, emb, normed, hid, proj, att, scores, wts,
    d_att, d_hid, live_cot, gsum, gsend, grecv, gt, tsend, trecv, rowg, rsend, rrecv,
    local_sem, y_s, x_s, c_s, w_r, e_s, e_r, g_s, g_r, t_s, t_r, b_s, b_r,
):
    rep = lax.axis_index("replica")
    tab = lax.axis_index("table")
    rows = w_hbm.shape[0]
    cols = cache_hbm.shape[0]
    seq = cot_ref.shape[0]

    def rep_at(i):
        return lax.rem(rep + i, reps)

    def tab_at(i):
        return lax.rem(tab + i, tabs)

    def row_block(r):
        return pl.ds(pl.multiple_of(r * rows, rows), rows)

    own_cache = pltpu.make_async_copy(cache_hbm, cache_v, local_sem.at[0])
    own_w = pltpu.make_async_copy(
        w_hbm, w_v.at[row_block(rep), pl.ds(0, 4 * D)], local_sem.at[1])
    own_wo = pltpu.make_async_copy(
        wo_hbm, w_v.at[row_block(rep), pl.ds(4 * D, D)], local_sem.at[2])
    own_w.start()
    own_wo.start()
    own_cache.start()

    barrier = pltpu.get_barrier_semaphore()

    @pl.loop(1, reps)
    def _(i):
        pl.semaphore_signal(barrier, inc=1, device_id={"replica": rep_at(i)})

    @pl.loop(1, tabs)
    def _(i):
        pl.semaphore_signal(barrier, inc=1, device_id={"table": tab_at(i)})

    pl.semaphore_wait(barrier, reps - 1 + tabs - 1)

    parity = lax.rem(tab, 2)
    side = lax.rem(rep, 2)
    mate = rep + 1 - 2 * side
    beside = tab + 1 - 2 * parity
    pairs = reps // 2
    pieces = 5 * D // PIECE
    steps = pieces // 2

    def piece(source, j):
        return w_v.at[row_block(source), pl.ds(pl.multiple_of(j * PIECE, PIECE), PIECE)]

    def other(i):
        return 2 * lax.rem(rep // 2 + i, pairs) + side

    def y_copy(to, source, j):
        return pltpu.make_async_remote_copy(
            src_ref=piece(source, j), dst_ref=piece(source, j),
            send_sem=y_s.at[to, j], recv_sem=w_r.at[source, j], device_id={"replica": to})

    def x_copy(source, j):
        return pltpu.make_async_remote_copy(
            src_ref=piece(source, j), dst_ref=piece(source, j),
            send_sem=x_s.at[source, j], recv_sem=w_r.at[source, j],
            device_id={"table": beside})

    def c_copy(source, j):
        return pltpu.make_async_remote_copy(
            src_ref=piece(source, j), dst_ref=piece(source, j),
            send_sem=c_s.at[source, j], recv_sem=w_r.at[source, j],
            device_id={"replica": mate})

    def order(step):
        return (step + 1) % (steps - 1) if step < steps - 1 else steps - 1

    def relay_direct(step):
        j = 2 * order(step) + parity

        @pl.loop(1, pairs)
        def _(i):
            source = other(i)
            y_copy(rep, source, j).wait_recv()
            x_copy(source, j).start()
            c_copy(source, j).start()

    def relay_beside(step):
        j = 2 * order(step) + 1 - parity

        @pl.loop(1, pairs)
        def _(i):
            source = other(i)
            x_copy(source, j).wait_recv()
            c_copy(source, j).start()

    def columns_ready(step):
        for k in range(2):
            @pl.loop(0, pairs)
            def _(i):
                source = 2 * i + 1 - side
                c_copy(source, 2 * order(step) + k).wait_recv()

    def g_copy(to, source):
        return pltpu.make_async_remote_copy(
            src_ref=gsend.at[row_block(to)], dst_ref=grecv.at[source],
            send_sem=g_s.at[to], recv_sem=g_r.at[source], device_id={"replica": to})

    def e_copy(to, source):
        return pltpu.make_async_remote_copy(
            src_ref=picked.at[to], dst_ref=arrived.at[source],
            send_sem=e_s.at[to], recv_sem=e_r.at[source], device_id={"table": to})

    def t_copy(to, source):
        return pltpu.make_async_remote_copy(
            src_ref=tsend.at[to], dst_ref=trecv.at[source],
            send_sem=t_s.at[to], recv_sem=t_r.at[source], device_id={"table": to})

    def b_copy(to, source):
        return pltpu.make_async_remote_copy(
            src_ref=rsend.at[to], dst_ref=rrecv.at[source],
            send_sem=b_s.at[to], recv_sem=b_r.at[source], device_id={"table": to})

    def start_rep(copy):
        @pl.loop(1, reps)
        def _(i):
            copy(rep_at(i), rep).start()

    def start_tab(copy):
        @pl.loop(1, tabs)
        def _(i):
            copy(tab_at(i), tab).start()

    def recv_tab(copy):
        @pl.loop(1, tabs)
        def _(i):
            copy(tab, tab_at(i)).wait_recv()

    own_w.wait()
    own_wo.wait()
    for step in range(steps):
        j = 2 * order(step) + parity

        @pl.loop(1, pairs)
        def _(i):
            y_copy(other(i), rep, j).start()

        c_copy(rep, 2 * order(step)).start()
        c_copy(rep, 2 * order(step) + 1).start()

    tab_slots = slots_ref.shape[1]

    def own_scalar(value):
        total = jnp.int32(0)
        for n in range(tab_slots):
            total = total + jnp.where(slots_ref[0, n] == tab, value(n), 0)
        return total

    length = own_scalar(lambda n: lengths_ref[0, n])
    width = seq // blocks
    at_i = lax.broadcasted_iota(jnp.int32, (seq, seq), 0)
    at_j = lax.broadcasted_iota(jnp.int32, (seq, seq), 1)
    pattern = jnp.zeros((seq, seq), jnp.int32)
    for a in range(blocks):
        for b in range(blocks):
            here = ((at_i >= a * width) & (at_i < (a + 1) * width)
                    & (at_j >= b * width) & (at_j < (b + 1) * width))
            chosen = 1 if a == b else own_scalar(lambda n: mask_ref[0, n, a, b])
            pattern = jnp.where(here, chosen, pattern)
    allowed = jnp.where((pattern > 0) & (at_j <= at_i) & (at_i < length), 1.0, 0.0)
    live = jnp.where(lax.broadcasted_iota(jnp.int32, (seq, D), 0) < length, 1.0, 0.0)
    cot = cot_ref[...].astype(F32) * live
    live_cot[...] = cot.astype(BF16)

    relay_direct(0)

    row_ids = row_ids_ref[0]
    at_slot = lax.broadcasted_iota(jnp.int32, row_ids.shape, 0)
    slot_rows = jnp.zeros_like(row_ids)
    for n in range(tab_slots):
        slot_rows = slot_rows + jnp.where(
            at_slot == slots_ref[0, n], row_ids[n : n + 1, :], 0)
    for q in range(tab_slots):
        ids_ref[:, q * seq : (q + 1) * seq] = slot_rows[q : q + 1, :]

    own_cache.wait()
    ids = ids_ref[...]
    size = min(CHUNK, cache_v.shape[1])
    found = jnp.zeros((cols, ids.shape[1]), F32)
    for m in range(0, cache_v.shape[1], size):
        found = found + mm(
            cache_v[:, m : m + size].astype(BF16), one_hot(ids, m, size), NN)
    for q in range(tabs):
        picked[q] = found[:, q * seq : (q + 1) * seq].astype(BF16)
    start_tab(e_copy)
    arrived[tab] = picked[tab]
    recv_tab(e_copy)
    for q in range(tabs):
        emb[q * cols : (q + 1) * cols, :] = arrived[q].astype(F32)

    e = emb[...]
    centred = e - jnp.mean(e, axis=0, keepdims=True)
    inverse = 1.0 / jnp.sqrt(jnp.mean(centred * centred, axis=0, keepdims=True) + EPS_NORM)
    norm = centred * inverse
    normed[...] = norm

    rows_normed = normed[...].T.astype(BF16)

    def project(step):
        columns_ready(step)
        at = pl.ds(pl.multiple_of(order(step) * 2 * PIECE, 2 * PIECE), 2 * PIECE)
        h = mm(rows_normed, w_v[:, at], NN)
        hid[:, at] = h
        proj[:, at] = (h / (1.0 + jnp.exp(-h))).astype(BF16)

    for step in range(1, steps + 2):
        if step < steps:
            relay_direct(step)
        if step - 1 < steps:
            relay_beside(step - 1)
        if 0 <= step - 2 < steps - 1:
            project(step - 2)

    lane = lax.broadcasted_iota(jnp.int32, (seq, PAIR), 1)
    halves = [lane < HEAD_DIM, lane >= HEAD_DIM]

    def half(x, k):
        return jnp.where(halves[k], x, jnp.zeros_like(x))

    scale = HEAD_DIM ** (-0.5)
    for p in range(HEADS // 2):
        at = p * PAIR
        q2 = proj[:, D + at : D + at + PAIR]
        k2 = proj[:, 2 * D + at : 2 * D + at + PAIR]
        v2 = proj[:, 3 * D + at : 3 * D + at + PAIR]
        total = None
        for k in range(2):
            s = mm(q2, half(k2, k), NT) * scale
            scores[2 * p + k] = s
            w = (s / (1.0 + jnp.exp(-s)) * allowed).astype(BF16)
            wts[2 * p + k] = w
            part = mm(w, half(v2, k), NN)
            total = part if total is None else total + part
        att[:, at : at + PAIR] = total

    a = att[...]
    c_att = a - jnp.mean(a, axis=1, keepdims=True)
    inv_att = 1.0 / jnp.sqrt(jnp.mean(c_att * c_att, axis=1, keepdims=True) + EPS_ATTN)
    y = c_att * inv_att
    gate = proj[:, :D].astype(F32)
    gated = (y * gate).astype(BF16)

    gsum[...] = mm(gated, live_cot[...], TN)
    gsend[...] = gsum[...].astype(BF16)
    start_rep(g_copy)

    columns_ready(steps - 1)
    d_gated = mm(live_cot[...], w_v[:, 4 * D :], NT)

    def silu_grad(v):
        sig = 1.0 / (1.0 + jnp.exp(-v))
        return sig * (1.0 + v * (1.0 - sig))

    def put(at, width_of, value):
        h = hid[:, at : at + width_of]
        d_hid[:, at : at + width_of] = (
            value.astype(BF16).astype(F32) * silu_grad(h)).astype(BF16)

    put(0, D, d_gated * y)
    d_y = d_gated * gate
    d_att[...] = (inv_att * (
        d_y - jnp.mean(d_y, axis=1, keepdims=True)
        - y * jnp.mean(d_y * y, axis=1, keepdims=True))).astype(BF16)

    for p in range(HEADS // 2):
        at = p * PAIR
        q2 = proj[:, D + at : D + at + PAIR]
        k2 = proj[:, 2 * D + at : 2 * D + at + PAIR]
        v2 = proj[:, 3 * D + at : 3 * D + at + PAIR]
        da2 = d_att[:, at : at + PAIR]
        dq = dk = dv = None
        for k in range(2):
            s = scores[2 * p + k]
            dw = mm(da2, half(v2, k), NT).astype(BF16).astype(F32)
            ds = (dw * allowed * silu_grad(s) * scale).astype(BF16)
            dv_k = mm(wts[2 * p + k], half(da2, k), TN)
            dq_k = mm(ds, half(k2, k), NN)
            dk_k = mm(ds, half(q2, k), TN)
            dq = dq_k if dq is None else dq + dq_k
            dk = dk_k if dk is None else dk + dk_k
            dv = dv_k if dv is None else dv + dv_k
        put(D + at, PAIR, dq)
        put(2 * D + at, PAIR, dk)
        put(3 * D + at, PAIR, dv)

    d_norm = mm(w_v[:, : 4 * D], d_hid[...], NT)
    e = emb[...]
    centred = e - jnp.mean(e, axis=0, keepdims=True)
    inverse = 1.0 / jnp.sqrt(jnp.mean(centred * centred, axis=0, keepdims=True) + EPS_NORM)
    norm = centred * inverse
    rowg[...] = live_cot[...].astype(F32).T + inverse * (
        d_norm - jnp.mean(d_norm, axis=0, keepdims=True)
        - norm * jnp.mean(d_norm * norm, axis=0, keepdims=True))
    for q in range(tabs):
        rsend[q] = rowg[q * cols : (q + 1) * cols, :].astype(BF16)
    start_tab(b_copy)
    rrecv[tab] = rsend[tab]

    summed = gsum[row_block(rep), :]
    for i in range(1, reps):
        source = rep_at(i)
        g_copy(rep, source).wait_recv()
        summed = summed + grecv[source].astype(F32)
    gt[...] = summed.T
    for q in range(tabs):
        tsend[q] = gt[q * cols : (q + 1) * cols, :].astype(BF16)
    start_tab(t_copy)
    trecv[tab] = tsend[tab]

    recv_tab(b_copy)
    back_ref[...] = rrecv[...]

    recv_tab(t_copy)
    out = trecv[0].astype(F32)
    for q in range(1, tabs):
        out = out + trecv[q].astype(F32)
    grad_ref[...] = out

    for step in range(steps):
        direct = 2 * order(step) + parity
        c_copy(rep, direct).wait_send()
        c_copy(rep, 2 * order(step) + 1 - parity).wait_send()

        @pl.loop(1, pairs)
        def _(i):
            y_copy(other(i), rep, direct).wait_send()
            x_copy(other(i), direct).wait_send()
            c_copy(other(i), direct).wait_send()
            c_copy(other(i), 2 * order(step) + 1 - parity).wait_send()

    @pl.loop(1, reps)
    def _(i):
        g_copy(rep_at(i), rep).wait_send()

    for copy in (e_copy, b_copy, t_copy):
        @pl.loop(1, tabs)
        def _(i):
            copy(tab_at(i), tab).wait_send()


def update_kernel(
    back_ref, ids_ref, grad_ref, w2_ref, cache_ref, accum_ref, cache_out, accum_out, w2_out, grads
):
    step = pl.program_id(0)
    tabs, _, seq = back_ref.shape
    size = cache_ref.shape[1]

    @pl.when(step == 0)
    def _():
        for q in range(tabs):
            grads[:, q * seq : (q + 1) * seq] = back_ref[q]
        summed = grad_ref[...].T
        w2_out[...] = summed * lax.rsqrt(w2_ref[...] + summed * summed)

    grad = mm(grads[...], one_hot(ids_ref[...], step * size, size), NT)
    accum_next = accum_ref[...] + grad * grad
    accum_out[...] = accum_next
    cache_out[...] = cache_ref[...] - STEP_SIZE * grad * lax.rsqrt(accum_next)


def body(cache, accum, row_ids, lengths, seq_slot, block_mask, cotangent, w_uqkv, w_out, w2_accum):
    reps = lax.axis_size("replica")
    tabs = lax.axis_size("table")
    cols, cached = cache.shape
    rows = w_uqkv.shape[0]
    seq = row_ids.shape[2]
    blocks = block_mask.shape[-1]
    slots = seq_slot.shape[1]

    vmem = pl.BlockSpec(memory_space=pltpu.VMEM)
    smem = pl.BlockSpec(memory_space=pltpu.SMEM)
    hbm = pl.BlockSpec(memory_space=pl.ANY)
    dma = pltpu.SemaphoreType.DMA
    V = pltpu.VMEM
    pieces = 5 * D // PIECE
    back, grad_t, ids = pl.pallas_call(
        functools.partial(layer_kernel, reps, tabs, blocks),
        out_shape=(
            jax.ShapeDtypeStruct((tabs, cols, seq), BF16),
            jax.ShapeDtypeStruct((cols, rows), F32),
            jax.ShapeDtypeStruct((1, slots * seq), jnp.int32),
        ),
        in_specs=[smem, smem, smem, hbm, vmem, vmem, hbm, hbm],
        out_specs=(vmem, vmem, vmem),
        scratch_shapes=[
            V((cols, cached), F32), V((D, 5 * D), BF16),
            V((tabs, cols, seq), BF16), V((tabs, cols, seq), BF16), V((D, seq), F32),
            V((D, seq), F32), V((seq, 4 * D), F32), V((seq, 4 * D), BF16),
            V((seq, D), F32), V((HEADS, seq, seq), F32), V((HEADS, seq, seq), BF16),
            V((seq, D), BF16), V((seq, 4 * D), BF16), V((seq, D), BF16),
            V((D, D), F32), V((D, D), BF16), V((reps, rows, D), BF16),
            V((D, rows), F32), V((tabs, cols, rows), BF16), V((tabs, cols, rows), BF16),
            V((D, seq), F32), V((tabs, cols, seq), BF16), V((tabs, cols, seq), BF16),
            dma((3,)), dma((reps, pieces)), dma((reps, pieces)), dma((reps, pieces)),
            dma((reps, pieces)),
            dma((tabs,)), dma((tabs,)), dma((reps,)), dma((reps,)),
            dma((tabs,)), dma((tabs,)), dma((tabs,)), dma((tabs,)),
        ],
        compiler_params=pltpu.CompilerParams(
            collective_id=0, has_side_effects=True, vmem_limit_bytes=56 * 1024 * 1024),
        name="layer",
    )(seq_slot, lengths, block_mask, cache, row_ids, cotangent[0], w_uqkv, w_out)

    size = min(CHUNK, cached)
    block = pl.BlockSpec((cols, size), lambda m: (0, m))
    cache_next, accum_next, w2_step = pl.pallas_call(
        update_kernel,
        grid=(cached // size,),
        out_shape=(jax.ShapeDtypeStruct(cache.shape, F32),) * 2
        + (jax.ShapeDtypeStruct(w2_accum.shape, F32),),
        in_specs=[
            pl.BlockSpec((tabs, cols, seq), lambda m: (0, 0, 0)),
            pl.BlockSpec((1, slots * seq), lambda m: (0, 0)),
            pl.BlockSpec((cols, rows), lambda m: (0, 0)),
            pl.BlockSpec((rows, cols), lambda m: (0, 0)),
            block, block,
        ],
        out_specs=(block, block, pl.BlockSpec((rows, cols), lambda m: (0, 0))),
        scratch_shapes=[V((cols, tabs * seq), BF16)],
        compiler_params=pltpu.CompilerParams(vmem_limit_bytes=40 * 1024 * 1024),
        name="update",
    )(back, ids, grad_t, w2_accum, cache, accum)

    return (cache_next, accum_next, w2_step)


def solution(mesh):
    return jax.shard_map(
        body,
        mesh=mesh,
        in_specs=(
            P("table", "replica"),
            P("table", "replica"),
            P("replica", None, None),
            P("replica", None),
            P("replica", None),
            P("replica", None, None, None),
            P("replica", "table", None),
            P("replica", None),
            P("replica", None),
            P("replica", "table"),
        ),
        out_specs=(P("table", "replica"), P("table", "replica"), P("replica", "table")),
        check_vma=False,
    )
```

```python
import functools

import jax
import jax.numpy as jnp
from jax import lax
from jax.experimental import pallas as pl
from jax.experimental.pallas import tpu as pltpu
from jax.sharding import PartitionSpec as P

D = 768
HEADS = 12
HEAD_DIM = 64
EPS_NORM = 1e-05
EPS_ATTN = 1e-06
STEP_SIZE = 0.5
PAIR = 2 * HEAD_DIM
CHUNK = 512
PIECE = D // 2

F32 = jnp.float32
BF16 = jnp.bfloat16

NN = (((1,), (0,)), ((), ()))
NT = (((1,), (1,)), ((), ()))
TN = (((0,), (0,)), ((), ()))


def mm(a, b, dims):
    return lax.dot_general(a, b, dims, preferred_element_type=F32)


def one_hot(ids, base, size):
    rows = lax.broadcasted_iota(jnp.int32, (size, ids.shape[1]), 0) + base
    return jnp.where(rows == ids, 1.0, 0.0).astype(BF16)


def layer_kernel(
    reps, tabs, blocks,
    slots_ref, lengths_ref, mask_ref, cache_hbm, row_ids_ref, cot_ref, w_hbm, wo_hbm,
    back_ref, grad_ref, ids_ref,
    cache_v, w_v, picked, arrived, emb, normed, hid, proj, att, scores, wts,
    d_att, d_hid, live_cot, gsum, gsend, crecv, ysend, yrecv, gt, tsend, trecv, rowg, rsend, rrecv,
    local_sem, y_s, x_s, c_s, w_r, e_s, e_r, m_s, m_r, g_s, g_r, t_s, t_r, b_s, b_r,
):
    rep = lax.axis_index("replica")
    tab = lax.axis_index("table")
    rows = w_hbm.shape[0]
    cols = cache_hbm.shape[0]
    seq = cot_ref.shape[0]

    def rep_at(i):
        return lax.rem(rep + i, reps)

    def tab_at(i):
        return lax.rem(tab + i, tabs)

    def row_block(r):
        return pl.ds(pl.multiple_of(r * rows, rows), rows)

    own_cache = pltpu.make_async_copy(cache_hbm, cache_v, local_sem.at[0])
    own_w = pltpu.make_async_copy(
        w_hbm, w_v.at[row_block(rep), pl.ds(0, 4 * D)], local_sem.at[1])
    own_wo = pltpu.make_async_copy(
        wo_hbm, w_v.at[row_block(rep), pl.ds(4 * D, D)], local_sem.at[2])
    own_w.start()
    own_wo.start()
    own_cache.start()

    barrier = pltpu.get_barrier_semaphore()

    @pl.loop(1, reps)
    def _(i):
        pl.semaphore_signal(barrier, inc=1, device_id={"replica": rep_at(i)})

    @pl.loop(1, tabs)
    def _(i):
        pl.semaphore_signal(barrier, inc=1, device_id={"table": tab_at(i)})

    pl.semaphore_wait(barrier, reps - 1 + tabs - 1)

    parity = lax.rem(tab, 2)
    side = lax.rem(rep, 2)
    mate = rep + 1 - 2 * side
    beside = tab + 1 - 2 * parity
    pairs = reps // 2
    pieces = 5 * D // PIECE
    steps = pieces // 2

    def piece(source, j):
        return w_v.at[row_block(source), pl.ds(pl.multiple_of(j * PIECE, PIECE), PIECE)]

    def other(i):
        return 2 * lax.rem(rep // 2 + i, pairs) + side

    def y_copy(to, source, j):
        return pltpu.make_async_remote_copy(
            src_ref=piece(source, j), dst_ref=piece(source, j),
            send_sem=y_s.at[to, j], recv_sem=w_r.at[source, j], device_id={"replica": to})

    def y_send(to, step):
        j = 2 * order(step) + parity
        if step < steps - 1:
            held, at = w_hbm, j
        else:
            held, at = wo_hbm, j - 2 * (steps - 1)
        return pltpu.make_async_remote_copy(
            src_ref=held.at[:, pl.ds(pl.multiple_of(at * PIECE, PIECE), PIECE)],
            dst_ref=piece(rep, j),
            send_sem=y_s.at[to, j], recv_sem=w_r.at[rep, j], device_id={"replica": to})

    def x_copy(source, j):
        return pltpu.make_async_remote_copy(
            src_ref=piece(source, j), dst_ref=piece(source, j),
            send_sem=x_s.at[source, j], recv_sem=w_r.at[source, j],
            device_id={"table": beside})

    def c_copy(source, j):
        return pltpu.make_async_remote_copy(
            src_ref=piece(source, j), dst_ref=piece(source, j),
            send_sem=c_s.at[source, j], recv_sem=w_r.at[source, j],
            device_id={"replica": mate})

    def order(step):
        return (step + 1) % (steps - 1) if step < steps - 1 else steps - 1

    def relay_direct(step):
        j = 2 * order(step) + parity

        @pl.loop(1, pairs)
        def _(i):
            source = other(i)
            y_copy(rep, source, j).wait_recv()
            x_copy(source, j).start()
            c_copy(source, j).start()

    def relay_beside(step):
        j = 2 * order(step) + 1 - parity

        @pl.loop(1, pairs)
        def _(i):
            source = other(i)
            x_copy(source, j).wait_recv()
            c_copy(source, j).start()

    def columns_ready(step):
        for k in range(2):
            @pl.loop(0, pairs)
            def _(i):
                source = 2 * i + 1 - side
                c_copy(source, 2 * order(step) + k).wait_recv()

    def m_copy(i):
        return pltpu.make_async_remote_copy(
            src_ref=gsend.at[row_block(2 * i + 1 - side)], dst_ref=crecv.at[i],
            send_sem=m_s.at[i], recv_sem=m_r.at[i], device_id={"replica": mate})

    def g_copy(to, source):
        return pltpu.make_async_remote_copy(
            src_ref=ysend.at[to], dst_ref=yrecv.at[source],
            send_sem=g_s.at[to], recv_sem=g_r.at[source],
            device_id={"replica": 2 * to + side})

    def e_copy(to, source):
        return pltpu.make_async_remote_copy(
            src_ref=picked.at[to], dst_ref=arrived.at[source],
            send_sem=e_s.at[to], recv_sem=e_r.at[source], device_id={"table": to})

    def t_copy(to, source):
        return pltpu.make_async_remote_copy(
            src_ref=tsend.at[to], dst_ref=trecv.at[source],
            send_sem=t_s.at[to], recv_sem=t_r.at[source], device_id={"table": to})

    def b_copy(to, source):
        return pltpu.make_async_remote_copy(
            src_ref=rsend.at[to], dst_ref=rrecv.at[source],
            send_sem=b_s.at[to], recv_sem=b_r.at[source], device_id={"table": to})

    def start_tab(copy):
        @pl.loop(1, tabs)
        def _(i):
            copy(tab_at(i), tab).start()

    def recv_tab(copy):
        @pl.loop(1, tabs)
        def _(i):
            copy(tab, tab_at(i)).wait_recv()

    for step in range(steps):
        @pl.loop(1, pairs)
        def _(i):
            y_send(other(i), step).start()

    own_w.wait()
    own_wo.wait()
    for step in range(steps):
        c_copy(rep, 2 * order(step)).start()
        c_copy(rep, 2 * order(step) + 1).start()

    tab_slots = slots_ref.shape[1]

    def own_scalar(value):
        total = jnp.int32(0)
        for n in range(tab_slots):
            total = total + jnp.where(slots_ref[0, n] == tab, value(n), 0)
        return total

    length = own_scalar(lambda n: lengths_ref[0, n])
    width = seq // blocks
    at_i = lax.broadcasted_iota(jnp.int32, (seq, seq), 0)
    at_j = lax.broadcasted_iota(jnp.int32, (seq, seq), 1)
    pattern = jnp.zeros((seq, seq), jnp.int32)
    for a in range(blocks):
        for b in range(blocks):
            here = ((at_i >= a * width) & (at_i < (a + 1) * width)
                    & (at_j >= b * width) & (at_j < (b + 1) * width))
            chosen = 1 if a == b else own_scalar(lambda n: mask_ref[0, n, a, b])
            pattern = jnp.where(here, chosen, pattern)
    allowed = jnp.where((pattern > 0) & (at_j <= at_i) & (at_i < length), 1.0, 0.0)
    live = jnp.where(lax.broadcasted_iota(jnp.int32, (seq, D), 0) < length, 1.0, 0.0)
    cot = cot_ref[...].astype(F32) * live
    live_cot[...] = cot.astype(BF16)

    relay_direct(0)

    row_ids = row_ids_ref[0]
    at_slot = lax.broadcasted_iota(jnp.int32, row_ids.shape, 0)
    slot_rows = jnp.zeros_like(row_ids)
    for n in range(tab_slots):
        slot_rows = slot_rows + jnp.where(
            at_slot == slots_ref[0, n], row_ids[n : n + 1, :], 0)
    for q in range(tab_slots):
        ids_ref[:, q * seq : (q + 1) * seq] = slot_rows[q : q + 1, :]

    own_cache.wait()
    ids = ids_ref[...]
    size = min(CHUNK, cache_v.shape[1])
    found = jnp.zeros((cols, ids.shape[1]), F32)
    for m in range(0, cache_v.shape[1], size):
        found = found + mm(
            cache_v[:, m : m + size].astype(BF16), one_hot(ids, m, size), NN)
    for q in range(tabs):
        picked[q] = found[:, q * seq : (q + 1) * seq].astype(BF16)
    start_tab(e_copy)
    arrived[tab] = picked[tab]
    recv_tab(e_copy)
    for q in range(tabs):
        emb[q * cols : (q + 1) * cols, :] = arrived[q].astype(F32)

    e = emb[...]
    centred = e - jnp.mean(e, axis=0, keepdims=True)
    inverse = 1.0 / jnp.sqrt(jnp.mean(centred * centred, axis=0, keepdims=True) + EPS_NORM)
    norm = centred * inverse
    normed[...] = norm

    rows_normed = normed[...].T.astype(BF16)

    def project(step):
        columns_ready(step)
        at = pl.ds(pl.multiple_of(order(step) * 2 * PIECE, 2 * PIECE), 2 * PIECE)
        h = mm(rows_normed, w_v[:, at], NN)
        hid[:, at] = h
        proj[:, at] = (h / (1.0 + jnp.exp(-h))).astype(BF16)

    lane = lax.broadcasted_iota(jnp.int32, (seq, PAIR), 1)
    halves = [lane < HEAD_DIM, lane >= HEAD_DIM]

    def half(x, k):
        return jnp.where(halves[k], x, jnp.zeros_like(x))

    scale = HEAD_DIM ** (-0.5)
    def attend(first, last):
        for p in range(first, last):
            at = p * PAIR
            q2 = proj[:, D + at : D + at + PAIR]
            k2 = proj[:, 2 * D + at : 2 * D + at + PAIR]
            v2 = proj[:, 3 * D + at : 3 * D + at + PAIR]
            total = None
            for k in range(2):
                s = mm(q2, half(k2, k), NT) * scale
                scores[2 * p + k] = s
                w = (s / (1.0 + jnp.exp(-s)) * allowed).astype(BF16)
                wts[2 * p + k] = w
                part = mm(w, half(v2, k), NN)
                total = part if total is None else total + part
            att[:, at : at + PAIR] = total

    middle = HEADS // 4
    for step in range(1, steps + 1):
        if step < steps:
            relay_direct(step)
        relay_beside(step - 1)
        if step < steps:
            project(step - 1)
        if step == steps - 2:
            attend(0, middle)
        if step == steps - 1:
            attend(middle, HEADS // 2)

    a = att[...]
    c_att = a - jnp.mean(a, axis=1, keepdims=True)
    inv_att = 1.0 / jnp.sqrt(jnp.mean(c_att * c_att, axis=1, keepdims=True) + EPS_ATTN)
    y = c_att * inv_att
    gate = proj[:, :D].astype(F32)
    gated = (y * gate).astype(BF16)

    gsum[...] = mm(gated, live_cot[...], TN)
    gsend[...] = gsum[...].astype(BF16)

    @pl.loop(0, pairs)
    def _(i):
        m_copy(i).start()


    columns_ready(steps - 1)
    d_gated = mm(live_cot[...], w_v[:, 4 * D :], NT)

    def silu_grad(v):
        sig = 1.0 / (1.0 + jnp.exp(-v))
        return sig * (1.0 + v * (1.0 - sig))

    def put(at, width_of, value):
        h = hid[:, at : at + width_of]
        d_hid[:, at : at + width_of] = (
            value.astype(BF16).astype(F32) * silu_grad(h)).astype(BF16)

    put(0, D, d_gated * y)
    d_y = d_gated * gate
    d_att[...] = (inv_att * (
        d_y - jnp.mean(d_y, axis=1, keepdims=True)
        - y * jnp.mean(d_y * y, axis=1, keepdims=True))).astype(BF16)

    @pl.loop(0, pairs)
    def _(i):
        m_copy(i).wait_recv()

    @pl.loop(1, pairs)
    def _(i):
        to = lax.rem(rep // 2 + i, pairs)
        ysend[to] = (gsum[row_block(2 * to + side), :] + crecv[to].astype(F32)).astype(BF16)
        g_copy(to, rep // 2).start()

    for p in range(HEADS // 2):
        at = p * PAIR
        q2 = proj[:, D + at : D + at + PAIR]
        k2 = proj[:, 2 * D + at : 2 * D + at + PAIR]
        v2 = proj[:, 3 * D + at : 3 * D + at + PAIR]
        da2 = d_att[:, at : at + PAIR]
        dq = dk = dv = None
        for k in range(2):
            s = scores[2 * p + k]
            dw = mm(da2, half(v2, k), NT).astype(BF16).astype(F32)
            ds = (dw * allowed * silu_grad(s) * scale).astype(BF16)
            dv_k = mm(wts[2 * p + k], half(da2, k), TN)
            dq_k = mm(ds, half(k2, k), NN)
            dk_k = mm(ds, half(q2, k), TN)
            dq = dq_k if dq is None else dq + dq_k
            dk = dk_k if dk is None else dk + dk_k
            dv = dv_k if dv is None else dv + dv_k
        put(D + at, PAIR, dq)
        put(2 * D + at, PAIR, dk)
        put(3 * D + at, PAIR, dv)

    d_norm = mm(w_v[:, : 4 * D], d_hid[...], NT)
    e = emb[...]
    centred = e - jnp.mean(e, axis=0, keepdims=True)
    inverse = 1.0 / jnp.sqrt(jnp.mean(centred * centred, axis=0, keepdims=True) + EPS_NORM)
    norm = centred * inverse
    rowg[...] = live_cot[...].astype(F32).T + inverse * (
        d_norm - jnp.mean(d_norm, axis=0, keepdims=True)
        - norm * jnp.mean(d_norm * norm, axis=0, keepdims=True))
    for q in range(tabs):
        rsend[q] = rowg[q * cols : (q + 1) * cols, :].astype(BF16)
    start_tab(b_copy)
    rrecv[tab] = rsend[tab]

    summed = gsum[row_block(rep), :] + crecv[rep // 2].astype(F32)
    for i in range(1, pairs):
        source = lax.rem(rep // 2 + i, pairs)
        g_copy(rep // 2, source).wait_recv()
        summed = summed + yrecv[source].astype(F32)
    gt[...] = summed.T
    for q in range(tabs):
        top = q * cols
        tsend[q, :, :rows] = gt[top : top + cols // 2, :].astype(BF16)
        tsend[q, :, rows:] = gt[top + cols // 2 : top + cols, :].astype(BF16)
    start_tab(t_copy)
    trecv[tab] = tsend[tab]

    recv_tab(b_copy)
    back_ref[...] = rrecv[...]

    recv_tab(t_copy)
    out = trecv[0].astype(F32)
    for q in range(1, tabs):
        out = out + trecv[q].astype(F32)
    grad_ref[: cols // 2, :] = out[:, :rows]
    grad_ref[cols // 2 :, :] = out[:, rows:]

    for step in range(steps):
        direct = 2 * order(step) + parity
        c_copy(rep, direct).wait_send()
        c_copy(rep, 2 * order(step) + 1 - parity).wait_send()

        @pl.loop(1, pairs)
        def _(i):
            y_send(other(i), step).wait_send()
            x_copy(other(i), direct).wait_send()
            c_copy(other(i), direct).wait_send()
            c_copy(other(i), 2 * order(step) + 1 - parity).wait_send()

    @pl.loop(0, pairs)
    def _(i):
        m_copy(i).wait_send()

    @pl.loop(1, pairs)
    def _(i):
        g_copy(lax.rem(rep // 2 + i, pairs), rep // 2).wait_send()

    for copy in (e_copy, b_copy, t_copy):
        @pl.loop(1, tabs)
        def _(i):
            copy(tab_at(i), tab).wait_send()


def update_kernel(
    back_ref, ids_ref, grad_ref, w2_ref, cache_ref, accum_ref, cache_out, accum_out, w2_out, grads
):
    step = pl.program_id(0)
    tabs, _, seq = back_ref.shape
    size = cache_ref.shape[1]

    @pl.when(step == 0)
    def _():
        for q in range(tabs):
            grads[:, q * seq : (q + 1) * seq] = back_ref[q]
        summed = grad_ref[...].T
        w2_out[...] = summed * lax.rsqrt(w2_ref[...] + summed * summed)

    grad = mm(grads[...], one_hot(ids_ref[...], step * size, size), NT)
    accum_next = accum_ref[...] + grad * grad
    accum_out[...] = accum_next
    cache_out[...] = cache_ref[...] - STEP_SIZE * grad * lax.rsqrt(accum_next)


def body(cache, accum, row_ids, lengths, seq_slot, block_mask, cotangent, w_uqkv, w_out, w2_accum):
    reps = lax.axis_size("replica")
    tabs = lax.axis_size("table")
    cols, cached = cache.shape
    rows = w_uqkv.shape[0]
    seq = row_ids.shape[2]
    blocks = block_mask.shape[-1]
    slots = seq_slot.shape[1]

    vmem = pl.BlockSpec(memory_space=pltpu.VMEM)
    smem = pl.BlockSpec(memory_space=pltpu.SMEM)
    hbm = pl.BlockSpec(memory_space=pl.ANY)
    dma = pltpu.SemaphoreType.DMA
    V = pltpu.VMEM
    pieces = 5 * D // PIECE
    back, grad_t, ids = pl.pallas_call(
        functools.partial(layer_kernel, reps, tabs, blocks),
        out_shape=(
            jax.ShapeDtypeStruct((tabs, cols, seq), BF16),
            jax.ShapeDtypeStruct((cols, rows), F32),
            jax.ShapeDtypeStruct((1, slots * seq), jnp.int32),
        ),
        in_specs=[smem, smem, smem, hbm, vmem, vmem, hbm, hbm],
        out_specs=(vmem, vmem, vmem),
        scratch_shapes=[
            V((cols, cached), F32), V((D, 5 * D), BF16),
            V((tabs, cols, seq), BF16), V((tabs, cols, seq), BF16), V((D, seq), F32),
            V((D, seq), F32), V((seq, 4 * D), F32), V((seq, 4 * D), BF16),
            V((seq, D), F32), V((HEADS, seq, seq), F32), V((HEADS, seq, seq), BF16),
            V((seq, D), BF16), V((seq, 4 * D), BF16), V((seq, D), BF16),
            V((D, D), F32), V((D, D), BF16), V((reps // 2, rows, D), BF16),
            V((reps // 2, rows, D), BF16), V((reps // 2, rows, D), BF16),
            V((D, rows), F32), V((tabs, cols // 2, 2 * rows), BF16),
            V((tabs, cols // 2, 2 * rows), BF16),
            V((D, seq), F32), V((tabs, cols, seq), BF16), V((tabs, cols, seq), BF16),
            dma((3,)), dma((reps, pieces)), dma((reps, pieces)), dma((reps, pieces)),
            dma((reps, pieces)),
            dma((tabs,)), dma((tabs,)), dma((reps // 2,)), dma((reps // 2,)),
            dma((reps // 2,)), dma((reps // 2,)),
            dma((tabs,)), dma((tabs,)), dma((tabs,)), dma((tabs,)),
        ],
        compiler_params=pltpu.CompilerParams(
            collective_id=0, has_side_effects=True, vmem_limit_bytes=56 * 1024 * 1024),
        name="layer",
    )(seq_slot, lengths, block_mask, cache, row_ids, cotangent[0], w_uqkv, w_out)

    size = min(CHUNK, cached)
    block = pl.BlockSpec((cols, size), lambda m: (0, m))
    cache_next, accum_next, w2_step = pl.pallas_call(
        update_kernel,
        grid=(cached // size,),
        out_shape=(jax.ShapeDtypeStruct(cache.shape, F32),) * 2
        + (jax.ShapeDtypeStruct(w2_accum.shape, F32),),
        in_specs=[
            pl.BlockSpec((tabs, cols, seq), lambda m: (0, 0, 0)),
            pl.BlockSpec((1, slots * seq), lambda m: (0, 0)),
            pl.BlockSpec((cols, rows), lambda m: (0, 0)),
            pl.BlockSpec((rows, cols), lambda m: (0, 0)),
            block, block,
        ],
        out_specs=(block, block, pl.BlockSpec((rows, cols), lambda m: (0, 0))),
        scratch_shapes=[V((cols, tabs * seq), BF16)],
        compiler_params=pltpu.CompilerParams(vmem_limit_bytes=62 * 1024 * 1024),
        name="update",
    )(back, ids, grad_t, w2_accum, cache, accum)

    return (cache_next, accum_next, w2_step)


def solution(mesh):
    return jax.shard_map(
        body,
        mesh=mesh,
        in_specs=(
            P("table", "replica"),
            P("table", "replica"),
            P("replica", None, None),
            P("replica", None),
            P("replica", None),
            P("replica", None, None, None),
            P("replica", "table", None),
            P("replica", None),
            P("replica", None),
            P("replica", "table"),
        ),
        out_specs=(P("table", "replica"), P("table", "replica"), P("replica", "table")),
        check_vma=False,
    )
```
